32 devices in a mesh: batch: 4 (over x, core), neuron: 8 (over z, y).
Axes of the slice: x: 2, y: 2, z: 4, core: 2. Of those that a mesh axis runs over, the one named last changes fastest.
Arguments:
- tokens: bfloat16 [2, 256, 12288], P(None, 'neuron', 'batch'), may hold values from -6 to 6
- ln_gain: float32 [12288], P('batch'), may hold values from 0.25 to 1.75
- ln_bias: float32 [12288], P('batch'), may hold values from -3 to 3
- up_weight: bfloat16 [12288, 24576], P('batch', 'neuron'), may hold values from -0.0546875 to 0.0546875
- up_bias: float32 [24576], P('neuron'), may hold values from -3 to 3
- down_weight: bfloat16 [24576, 12288], P('neuron', 'batch'), may hold values from -0.078125 to 0.078125
- down_bias: float32 [12288], P('batch'), may hold values from -3 to 3
- active: int32 [2, 2, 48], replicated, may hold values from 0 to 191, all different within a row
Outputs:
- mixed: bfloat16 [2, 256, 12288], P(None, 'neuron', 'batch')
The draws below stay inside these ranges and needn't reach their ends.
Inputs may be any that keep to these rules, and one draw needn't show every extreme that they name: `active`: each row block of each; despite its name it splits features, not a batch step lists 48 distinct neuron block numbers; every number appears in some list.
All inputs are finite; a program needn't handle non-finite values.
Results may differ from the reference program's by a relative error of at most 0.0044.
Values may be sent and summed in bfloat16 or wider, within the bound.
No kernel may reach another device: no remote copies, remote signals or barrier semaphores. Data moves between devices by JAX's collectives and lax.ppermute only.
A program may use at most 128 MiB of HBM per device.

```python
import jax
import jax.numpy as jnp
from jax import lax

D = 12288
FF = 24576
BLK = 128
RB = 128
K = 48
STEPS = 2
ROWS = 256
NB = 192
NRB = 2


def block_scale(key, extent, split, low, largest):
    gain = 1.0
    for position, blocks in split:
        heights = jax.random.uniform(jax.random.fold_in(jax.random.fold_in(key, 6), position), (blocks,), jnp.float32, low / len(split), largest / len(split))
        gain = gain * jnp.repeat(jnp.exp(heights), extent[position] // blocks).reshape((-1,) + (1,) * (len(extent) - 1 - position))
    return gain


def picks_of(stream_key, rows, number_of, top, lift):
    sequence = jax.random.permutation(jax.random.fold_in(stream_key, 1), number_of)
    boost = sequence
    for power in range(3):
        boost = boost * boost // number_of
    boost = boost * lift // number_of
    chance = jax.random.randint(jax.random.fold_in(stream_key, 2), (rows, number_of), 0, 4096) + boost
    holders = jax.random.permutation(jax.random.fold_in(stream_key, 3), rows)[jnp.arange(number_of) % rows]
    chance = jnp.where(jnp.arange(rows)[:, None] == holders[None, :], 1 << 14, chance)
    priority = chance * number_of + jnp.arange(number_of)
    return lax.top_k(priority.astype(jnp.int32), top)[1].astype(jnp.int32)


def normal_values(rng, extent, scale, bound, shards=(), kind=jnp.bfloat16):
    result = jax.random.normal(rng, extent, jnp.float32) * scale
    if len(shards) > 0:
        result = block_scale(rng, extent, shards, -0.22, 0.18) * result
    return jnp.clip(result, min=-bound, max=bound).astype(kind)


def setup_inputs(seed: int = 0) -> dict:
    key_of = jax.random.split(jax.random.key(seed), 9)
    return {
        "tokens": normal_values(key_of[0], (STEPS, ROWS, D), 1.0, 6.0, ((1, 8), (2, 4))),
        "ln_gain": jnp.clip(1.0 + 0.15 * jax.random.normal(key_of[1], (D,), jnp.float32), 0.25, 1.75),
        "ln_bias": normal_values(key_of[2], (D,), 0.5, 3.0, ((0, 4),), jnp.float32),
        "up_weight": normal_values(key_of[3], (D, FF), D ** -0.5, 0.0546875, ((0, 4), (1, 8))),
        "up_bias": normal_values(key_of[4], (FF,), 0.5, 3.0, ((0, 8),), jnp.float32),
        "down_weight": normal_values(key_of[5], (FF, D), (K * BLK) ** -0.5, 0.078125, ((0, 8), (1, 4))),
        "down_bias": normal_values(key_of[6], (D,), 0.5, 3.0, ((0, 4),), jnp.float32),
        "active": picks_of(key_of[7], STEPS * NRB, NB, K, 2048).reshape((STEPS, NRB, K)),
    }


epsilon = 1e-05

def block_table(listed):
    block_ids = jnp.arange(NB, dtype=jnp.int32)
    return jnp.any(listed[:, :, None] == block_ids[None, None, :], axis=1).astype(jnp.float32)

def reference(tokens, ln_gain, ln_bias, up_weight, up_bias, down_weight, down_bias, active):
    results = []
    for step_index in range(STEPS):
        inputs = tokens[step_index].astype(jnp.float32)
        average = lax.optimization_barrier(jnp.mean(inputs, axis=-1, keepdims=True))
        spread = lax.optimization_barrier(jnp.mean(inputs * inputs, axis=-1, keepdims=True)) - average * average
        normed = ((inputs - average) * lax.rsqrt(spread + epsilon) * ln_gain + ln_bias).astype(jnp.bfloat16)
        preact = jnp.dot(normed, up_weight, preferred_element_type=jnp.float32) + up_bias
        table = block_table(active[step_index])
        full_mask = jnp.repeat(jnp.repeat(table, RB, axis=0), BLK, axis=1)
        hidden = (jnp.maximum(preact, 0.0) * full_mask).astype(jnp.bfloat16)
        mixed = jnp.dot(hidden, down_weight, preferred_element_type=jnp.float32) + inputs + down_bias
        results.append(mixed.astype(jnp.bfloat16))
    return jnp.stack(results)
```

```python
import functools

import jax
import jax.numpy as jnp
from jax import lax
from jax.experimental import pallas as pl
from jax.experimental.pallas import tpu as pltpu
from jax.sharding import PartitionSpec as P

BLK = 128
RB = 128
CORES = 2
EPSILON = 1e-05
BUFFERS = 3
F32 = jnp.float32
BF16 = jnp.bfloat16
ANY = pl.BlockSpec(memory_space=pl.ANY)
SMEM = pl.BlockSpec(memory_space=pltpu.SMEM)
VMEM = pl.BlockSpec(memory_space=pltpu.VMEM)


def ring_order(mesh):
    devices = mesh.devices[0] if mesh.axis_names[0] == "batch" else mesh.devices[:, 0]
    count = len(devices)
    points = [tuple(getattr(d, "coords", (0, 0, i))) for i, d in enumerate(devices)]
    axes = [a for a in range(3) if len({p[a] for p in points}) > 1]
    if len(axes) != 2:
        return list(range(count))
    for first, second in (axes, axes[::-1]):
        rows = sorted({p[first] for p in points})
        columns = sorted({p[second] for p in points})
        if len(rows) % 2 == 0:
            break
    at = {(p[first], p[second]): i for i, p in enumerate(points)}
    walk = []
    for position, row in enumerate(rows):
        inner = columns if position == 0 else columns[1:]
        walk += [(row, column) for column in (inner if position % 2 == 0 else inner[::-1])]
    walk += [(row, columns[0]) for row in rows[:0:-1]]
    return [at[point] for point in walk]


def table_kernel(lists, picks, limit, first_ref, active_ref, block_ref, item_ref, count_ref):
    first = first_ref[0]

    def per_list(index, carry):
        slot, item = carry

        def per_pick(pick, slot):
            block = active_ref[index * picks + pick] - first
            block_ref[slot] = block
            return slot + jnp.where((block >= 0) & (block < limit[0]), 1, 0)

        end = lax.fori_loop(0, picks, per_pick, slot)

        def per_pair(pair, item):
            left = slot + 2 * pair
            item_ref[0, item] = index
            item_ref[1, item] = left
            item_ref[2, item] = jnp.where(left + 1 < end, left + 1, limit[1])
            return item + 1

        item = lax.fori_loop(0, (end - slot + 1) // 2, per_pair, item)
        return end, item

    slot, item = lax.fori_loop(0, lists, per_list, (0, 0))
    count_ref[0] = item
    count_ref[1] = slot


def make_tables(active, first_block, local_blocks, capacity):
    steps, row_blocks, picks = active.shape
    lists = steps * row_blocks
    return pl.pallas_call(
        functools.partial(table_kernel, lists, picks, (local_blocks, capacity)),
        out_shape=(
            jax.ShapeDtypeStruct((capacity + 1,), jnp.int32),
            jax.ShapeDtypeStruct((3, capacity + lists), jnp.int32),
            jax.ShapeDtypeStruct((2,), jnp.int32),
        ),
        in_specs=[SMEM, SMEM],
        out_specs=(SMEM, SMEM, SMEM),
        name="tables",
    )(first_block.reshape(1), active.reshape(-1))


def up_kernel(pieces_count, row_blocks, half, *refs):
    place_ref, core_ref, block_ref, item_ref, count_ref, weight_ref = refs[:6]
    pieces = refs[6 : 6 + pieces_count]
    keep_ref, send_ref, rows_ref, weights, total, row_sem, weight_sem = refs[6 + pieces_count :]
    shards = RB // rows_ref.shape[2]
    items = count_ref[0]

    def weight_copies(item):
        buffer = lax.rem(item, BUFFERS)
        left = item_ref[1, item]
        right = item_ref[2, item]
        right = jnp.where(right < 2 * half, right, left)
        return [
            pltpu.make_async_copy(
                weight_ref.at[:, pl.ds(pl.multiple_of(block_ref[slot] * BLK, BLK), BLK)],
                weights.at[buffer, :, pl.ds(side * BLK, BLK)],
                weight_sem.at[buffer, side],
            )
            for side, slot in enumerate((left, right))
        ]

    row_copies = [
        pltpu.make_async_copy(piece, rows_ref.at[index], row_sem.at[index])
        for index, piece in enumerate(pieces)
    ]
    for copy in row_copies:
        copy.start()
    for ahead in range(BUFFERS - 1):

        @pl.when(ahead < items)
        def _():
            for copy in weight_copies(ahead):
                copy.start()

    for copy in row_copies:
        copy.wait()

    def per_item(item, carry):
        @pl.when(item + BUFFERS - 1 < items)
        def _():
            for copy in weight_copies(item + BUFFERS - 1):
                copy.start()

        for copy in weight_copies(item):
            copy.wait()
        index = item_ref[0, item]
        step = index // row_blocks
        first = (index - step * row_blocks) * shards
        rows = jnp.concatenate(
            [rows_ref[place_ref[first + shard], step] for shard in range(shards)], axis=0
        )
        result = jnp.dot(rows, weights[lax.rem(item, BUFFERS)], preferred_element_type=F32)
        total[item_ref[1, item]] = result[:, :BLK]
        total[item_ref[2, item]] = result[:, BLK:]
        return carry

    lax.fori_loop(0, items, per_item, 0)
    mine = core_ref[0] * half
    keep_ref[...] = total[pl.ds(mine, half)]
    send_ref[...] = total[pl.ds(half - mine, half)].astype(BF16)


def up_project(place, core, tables, weight, pieces, row_blocks, capacity):
    half = capacity // CORES
    steps, shard_rows, width = pieces[0].shape
    return pl.pallas_call(
        functools.partial(up_kernel, len(pieces), row_blocks, half),
        out_shape=(
            jax.ShapeDtypeStruct((half, RB, BLK), F32),
            jax.ShapeDtypeStruct((half, RB, BLK), BF16),
        ),
        in_specs=[SMEM] * 5 + [ANY] * (1 + len(pieces)),
        out_specs=(VMEM, VMEM),
        scratch_shapes=[
            pltpu.VMEM((len(pieces), steps, shard_rows, width), BF16),
            pltpu.VMEM((BUFFERS, width, 2 * BLK), BF16),
            pltpu.VMEM((capacity + 1, RB, BLK), F32),
            pltpu.SemaphoreType.DMA((len(pieces),)),
            pltpu.SemaphoreType.DMA((BUFFERS, 2)),
        ],
        compiler_params=pltpu.CompilerParams(vmem_limit_bytes=40 << 20),
        cost_estimate=pl.CostEstimate(
            flops=2 * capacity * RB * BLK * width,
            bytes_accessed=capacity * BLK * width * 2,
            transcendentals=0,
        ),
        name="up",
    )(place, core, *tables, weight, *pieces)


def down_kernel(row_blocks, half, *refs):
    place_ref, core_ref, block_ref, item_ref, count_ref, weight_ref, own_ref, other_ref = refs[:8]
    far_ref, chain_ref, give_ref, home_ref = refs[8:12]
    hidden, weights, total, parts, hidden_sem, weight_sem, out_sem = refs[12:]
    shard_rows = parts.shape[2]
    shards = RB // shard_rows
    width = parts.shape[3]
    items = count_ref[0]
    mine = core_ref[0] * half

    def weight_copies(item):
        buffer = lax.rem(item, BUFFERS)
        left = item_ref[1, item]
        right = item_ref[2, item]
        right = jnp.where(right < 2 * half, right, left)
        return [
            pltpu.make_async_copy(
                weight_ref.at[pl.ds(pl.multiple_of(block_ref[slot] * BLK, BLK), BLK), :],
                weights.at[buffer, pl.ds(side * BLK, BLK), :],
                weight_sem.at[buffer, side],
            )
            for side, slot in enumerate((left, right))
        ]

    hidden_copies = [
        pltpu.make_async_copy(own_ref, hidden.at[pl.ds(mine, half)], hidden_sem.at[0]),
        pltpu.make_async_copy(other_ref, hidden.at[pl.ds(half - mine, half)], hidden_sem.at[1]),
    ]
    for copy in hidden_copies:
        copy.start()
    for ahead in range(BUFFERS - 1):

        @pl.when(ahead < items)
        def _():
            for copy in weight_copies(ahead):
                copy.start()

    hidden[2 * half] = jnp.zeros((RB, BLK), BF16)
    parts[...] = jnp.zeros(parts.shape, BF16)
    for copy in hidden_copies:
        copy.wait()

    def per_item(item, carry):
        @pl.when(item + BUFFERS - 1 < items)
        def _():
            for copy in weight_copies(item + BUFFERS - 1):
                copy.start()

        for copy in weight_copies(item):
            copy.wait()
        index = item_ref[0, item]
        before = item_ref[0, jnp.maximum(item - 1, 0)]
        after = item_ref[0, jnp.minimum(item + 1, items - 1)]
        opens = (item == 0) | (before != index)
        closes = (item == items - 1) | (after != index)
        values = jnp.concatenate([hidden[item_ref[1, item]], hidden[item_ref[2, item]]], axis=1)
        buffer = lax.rem(item, BUFFERS)
        piece = 512 if width % 512 == 0 else BLK

        @pl.when(opens)
        def _():
            for start in range(0, width, piece):
                total[:, start : start + piece] = jnp.dot(
                    values,
                    weights[buffer, :, start : start + piece],
                    preferred_element_type=F32,
                )

        @pl.when(jnp.logical_not(opens))
        def _():
            for start in range(0, width, piece):
                total[:, start : start + piece] += jnp.dot(
                    values,
                    weights[buffer, :, start : start + piece],
                    preferred_element_type=F32,
                )

        @pl.when(closes)
        def _():
            step = index // row_blocks
            first = (index - step * row_blocks) * shards
            for shard in range(shards):
                parts[place_ref[first + shard], step] = total[
                    shard * shard_rows : (shard + 1) * shard_rows
                ].astype(BF16)

        return carry

    lax.fori_loop(0, items, per_item, 0)
    count = chain_ref.shape[0]
    outs = [
        pltpu.make_async_copy(parts.at[0], home_ref, out_sem.at[0]),
        pltpu.make_async_copy(parts.at[2 * count + 1], far_ref, out_sem.at[1]),
    ]
    for k in range(1, count + 1):
        outs.append(
            pltpu.make_async_copy(parts.at[2 * k], chain_ref.at[k - 1], out_sem.at[2 * k])
        )
        outs.append(
            pltpu.make_async_copy(parts.at[2 * k - 1], give_ref.at[k - 1], out_sem.at[2 * k + 1])
        )
    for copy in outs:
        copy.start()
    for copy in outs:
        copy.wait()


def down_project(place, core, tables, weight, own, other, shape, ring, row_blocks, capacity):
    half = capacity // CORES
    steps, shard_rows, width = shape
    count = ring // 2 - 1
    return pl.pallas_call(
        functools.partial(down_kernel, row_blocks, half),
        out_shape=(
            jax.ShapeDtypeStruct(shape, BF16),
            jax.ShapeDtypeStruct((count,) + shape, BF16),
            jax.ShapeDtypeStruct((count,) + shape, BF16),
            jax.ShapeDtypeStruct(shape, BF16),
        ),
        in_specs=[SMEM] * 5 + [ANY] * 3,
        out_specs=(ANY,) * 4,
        scratch_shapes=[
            pltpu.VMEM((capacity + 1, RB, BLK), BF16),
            pltpu.VMEM((BUFFERS, 2 * BLK, width), BF16),
            pltpu.VMEM((RB, width), F32),
            pltpu.VMEM((ring,) + shape, BF16),
            pltpu.SemaphoreType.DMA((2,)),
            pltpu.SemaphoreType.DMA((BUFFERS, 2)),
            pltpu.SemaphoreType.DMA((ring,)),
        ],
        compiler_params=pltpu.CompilerParams(vmem_limit_bytes=40 << 20),
        cost_estimate=pl.CostEstimate(
            flops=2 * capacity * RB * BLK * width,
            bytes_accessed=capacity * BLK * width * 2,
            transcendentals=0,
        ),
        name="down",
    )(place, core, *tables, weight, own, other)


def solution(mesh):
    batch = mesh.shape["batch"]
    ring = mesh.shape["neuron"]
    order = ring_order(mesh)
    position_of = [order.index(n) for n in range(ring)]
    pair = [(b, b ^ 1) for b in range(batch)]
    chips = batch // CORES
    hop = [
        (b * ring + order[p], b * ring + order[(p + (1 if b % CORES == 0 else -1)) % ring])
        for b in range(batch)
        for p in range(ring)
    ]

    def to_partner(value):
        return lax.ppermute(value, "batch", pair)

    def onward(value):
        return lax.ppermute(value, ("batch", "neuron"), hop)

    def over_chips(value):
        return [
            lax.ppermute(
                value,
                "batch",
                [
                    (x * CORES + c, (x + d) % chips * CORES + c)
                    for x in range(chips)
                    for c in range(CORES)
                ],
            )
            for d in range(1, chips)
        ]

    def local(tokens, ln_gain, ln_bias, up_weight, up_bias, down_weight, down_bias, active):
        steps, shard_rows, width = tokens.shape
        _, row_blocks, picks = active.shape
        lists = steps * row_blocks
        local_blocks = up_weight.shape[1] // BLK
        all_blocks = local_blocks * ring
        capacity = min(local_blocks * lists, lists * picks - (all_blocks - local_blocks))
        capacity += capacity % CORES
        half = capacity // CORES
        model = width * batch
        far = ring // 2

        neuron_index = lax.axis_index("neuron")
        core = lax.axis_index("batch") % CORES
        here = jnp.array(position_of, jnp.int32)[neuron_index]
        away = (jnp.array(position_of, jnp.int32) - here) % ring
        away = jnp.where(core == 0, (ring - away) % ring, away)
        place = jnp.where(
            away == 0,
            0,
            jnp.where(
                away < far, 2 * away - 1, jnp.where(away == far, ring - 1, 2 * (ring - away))
            ),
        ).astype(jnp.int32)
        core = core.astype(jnp.int32).reshape(1)
        tables = make_tables(
            active, (neuron_index * local_blocks).astype(jnp.int32), local_blocks, capacity
        )

        wide = tokens.astype(F32)
        sums = jnp.stack([jnp.sum(wide, axis=-1), jnp.sum(wide * wide, axis=-1)])
        sums = sums + to_partner(sums)
        sums = sum(over_chips(sums), sums)
        average = sums[0] / model
        spread = sums[1] / model - average * average
        normed = (
            (wide - average[..., None]) * lax.rsqrt(spread + EPSILON)[..., None] * ln_gain
            + ln_bias
        ).astype(BF16)

        partner = to_partner(normed)
        gathered = [[] for _ in range(ring)]
        for step in range(steps):
            gathered[0].append(normed[step])
            message = jnp.stack([normed[step], partner[step]])
            for k in range(1, far):
                message = onward(message)
                gathered[2 * k - 1].append(message[0])
                gathered[2 * k].append(to_partner(message[1]))
            gathered[ring - 1].append(onward(message[0]))
        pieces = [jnp.stack(piece) for piece in gathered]

        keep, send = up_project(place, core, tables, up_weight, pieces, row_blocks, capacity)
        chip_sum = keep + to_partner(send).astype(F32)
        preact = sum((v.astype(F32) for v in over_chips(chip_sum.astype(BF16))), chip_sum)
        slots = lax.dynamic_slice_in_dim(tables[0], core[0] * half, half)
        bias = up_bias.reshape(local_blocks, BLK)[slots]
        hidden = jnp.maximum(preact + bias[:, None, :], 0.0).astype(BF16)
        hidden_other = to_partner(hidden)

        far_part, chain, give, home = down_project(
            place,
            core,
            tables,
            down_weight,
            hidden,
            hidden_other,
            tokens.shape,
            ring,
            row_blocks,
            capacity,
        )
        taken = to_partner(give)
        results = []
        for step in range(steps):
            moving = onward(far_part[step])
            for k in range(far - 1, 0, -1):
                mine = chain[k - 1, step].astype(F32)
                others = taken[k - 1, step].astype(F32)
                if k == far - 1:
                    message = jnp.stack([moving.astype(F32) + mine, others])
                else:
                    message = moving.astype(F32) + jnp.stack([mine, others])
                moving = onward(message.astype(BF16))
            rest = to_partner(moving[1])
            results.append(
                (
                    home[step].astype(F32)
                    + moving[0].astype(F32)
                    + rest.astype(F32)
                    + wide[step]
                    + down_bias
                ).astype(BF16)
            )
        return jnp.stack(results)

    in_specs = (
        P(None, "neuron", "batch"),
        P("batch"),
        P("batch"),
        P("batch", "neuron"),
        P("neuron"),
        P("neuron", "batch"),
        P("batch"),
        P(),
    )
    out_specs = P(None, "neuron", "batch")
    return jax.shard_map(local, mesh=mesh, in_specs=in_specs, out_specs=out_specs, check_vma=False)
```
